32 devices in a mesh: mem: 4 (over x, core), tile: 8 (over z, y).
Axes of the slice: x: 2, y: 2, z: 4, core: 2. Of those that a mesh axis runs over, the one named last changes fastest.
Arguments:
- ensemble: bfloat16 [512, 8, 1024], P('mem', None, 'tile'), may hold values from -6 to 6
- sweep_cfl_ratios: float32 [2, 8], replicated, may hold values from 0.05 to 0.45
- obs_cell: int32 [4, 1024], P('mem', 'tile'), may hold values from 0 to 255, as said below
- measurements_per_block: int32 [4, 8], P('mem', 'tile'), may hold values from 1 to 128, as said below
- obs_value: float32 [4, 1024], P('mem', 'tile'), may hold values from -8 to 8
- obs_weight: float32 [4, 1024], P('mem', 'tile'), may hold values from 1 to 10
Outputs:
- forecast: bfloat16 [512, 8, 1024], P('mem', None, 'tile')
The draws below stay inside these ranges and needn't reach their ends.
Inputs may be any that keep to these rules, and one draw needn't show every extreme that they name: `obs_cell`: slot o of block (b, t) names the cell r * 128 + c of its patch, which is grid row b * 2 + r and grid column t * 128 + c; the slots of one block name distinct cells. `measurements_per_block`: slots at or after a block's count are not in use; some block uses all 128 slots.
All inputs are finite; a program needn't handle non-finite values.
Results may differ from the reference program's by a relative error of at most 0.0025.
The reference program's roundings to bfloat16 on the way count: a program that leaves them out, or rounds other values in their place, can miss the bound.
Values may be sent and summed in bfloat16 or wider, within the bound.
A program may use at most 64 MiB of HBM per device.

```python
import math
import jax
import jax.numpy as jnp
from jax import lax

K = 512
NY = 8
BX = 128
OBS = 128
NS_ITERS = 2
BANDS = 4
TILES = 8
NYB = 2
NX = 1024
N_MEM = 4
N_TILE = 8


def draw_obs_cell(key, part):
    block_total = BANDS * TILES
    keys = jax.random.split(key, block_total)
    chosen = jax.vmap(lambda single: jax.random.permutation(single, NYB * BX)[:OBS])(keys)
    return chosen.astype(jnp.int32).reshape(BANDS, TILES * OBS)


def draw_measurements_per_block(key, part):
    block_total = BANDS * TILES
    uniform_draw = jax.random.randint(key, (block_total,), 0, OBS)
    counts = 1 + uniform_draw * uniform_draw // OBS
    fullest = jax.random.randint(jax.random.fold_in(key, 7), (), 0, block_total)
    counts = jnp.where(jnp.arange(block_total) == fullest, OBS, counts)
    return counts.astype(jnp.int32).reshape(BANDS, TILES)


def shard_levels(rng, dims, shards, smallest, top_value):
    loudness, own = 1.0, jax.random.fold_in(rng, 6)
    for position, shards_of in shards:
        steps = jnp.exp(jax.random.uniform(jax.random.fold_in(own, position), (shards_of,), jnp.float32, smallest / len(shards), top_value / len(shards)))
        loudness = loudness * jnp.repeat(steps, dims[position] // shards_of).reshape([-1 if axis == position else 1 for axis in range(len(dims))])
    return loudness


def bell_draw(own_key, extent, spread, most, pieces=(), held_as=jnp.bfloat16):
    factor_of = shard_levels(own_key, extent, pieces, -0.22, 0.18) if pieces else 1.0
    drawn = jax.random.normal(own_key, extent, jnp.float32) * spread * factor_of
    return jnp.minimum(jnp.maximum(drawn, -most), most).astype(held_as)


def setup_inputs(seed: int = 0) -> dict:
    seeds = jax.random.split(jax.random.key(seed), 7)
    ensemble = bell_draw(seeds[0], (K, NY, NX), 1.0, 6.0, ((0, 4), (2, 8)))
    sweep_cfl_ratios = jnp.clip(jax.random.uniform(seeds[1], (2, NY), jnp.float32, 0.05, 0.45), 0.05, 0.45)
    obs_cell = draw_obs_cell(jax.random.fold_in(seeds[6], 71), 0)
    measurements_per_block = draw_measurements_per_block(jax.random.fold_in(seeds[6], 71), 0)
    obs_value = bell_draw(seeds[4], (BANDS, TILES * OBS), 1.5, 8.0, ((0, 4), (1, 8)), jnp.float32)
    obs_weight = jnp.clip(jnp.exp(math.log(10.0) - 2.3025851 * jax.random.uniform(seeds[5], (BANDS, TILES * OBS), jnp.float32) ** shard_levels(seeds[5], (BANDS, TILES * OBS), ((0, 4), (1, 8)), -0.2, 0.2)), 1.0, 10.0)
    return dict(ensemble=ensemble, sweep_cfl_ratios=sweep_cfl_ratios, obs_cell=obs_cell, measurements_per_block=measurements_per_block, obs_value=obs_value, obs_weight=obs_weight)


def minmod(ahead, behind):
    smaller = jnp.where(jnp.abs(ahead) < jnp.abs(behind), ahead, behind)
    return jnp.where(ahead * behind > 0.0, smaller, 0.0)

def sweep_along(member_grids, sweep_cfl_ratios):
    ahead = jnp.roll(member_grids, -1, 2) - member_grids
    behind = member_grids - jnp.roll(member_grids, 1, 2)
    number = sweep_cfl_ratios[0][None, :, None]
    flux_values = number * (member_grids + 0.5 * (1.0 - number) * minmod(ahead, behind))
    return member_grids - (flux_values - jnp.roll(flux_values, 1, 2))

def sweep_across(member_grids, sweep_cfl_ratios):
    ahead = jnp.roll(member_grids, -1, 1) - member_grids
    behind = member_grids - jnp.roll(member_grids, 1, 1)
    number = sweep_cfl_ratios[1][None, :, None]
    flux_values = number * (member_grids + 0.5 * (1.0 - number) * minmod(ahead, behind))
    return member_grids - (flux_values - jnp.roll(flux_values, 1, 1))

def advance(member_grids, sweep_cfl_ratios):
    return sweep_across(sweep_along(member_grids, sweep_cfl_ratios), sweep_cfl_ratios)

def observe(local_domain_grid_points, obs_slots, obs_total, obs_values, obs_weights, tile_width):
    places = jnp.arange(local_domain_grid_points.shape[1], dtype=jnp.int32)
    picker = (places[:, None] == obs_slots[None, :]).astype(jnp.bfloat16)
    sampled = jnp.dot(local_domain_grid_points, picker, preferred_element_type=jnp.float32)
    sample_mean = lax.optimization_barrier(jnp.mean(sampled, axis=0))
    ensemble_dispersion = (sampled - sample_mean[None, :]).astype(jnp.bfloat16)
    innovation = (obs_values - sample_mean).astype(jnp.bfloat16)
    live_slot = jnp.arange(obs_slots.shape[0], dtype=jnp.int32) < obs_total
    weighted = jnp.where(live_slot, obs_weights, 0.0).astype(jnp.bfloat16)
    column = (obs_slots % tile_width).astype(jnp.bfloat16)
    return jnp.concatenate([ensemble_dispersion, innovation[None, :], weighted[None, :], column[None, :]], 0)

def split_parts(values):
    high = lax.optimization_barrier(values.astype(jnp.bfloat16))
    low = (values - high.astype(jnp.float32)).astype(jnp.bfloat16)
    return (high, low)

def newton_schulz(normalised_rows, identity):
    growing = normalised_rows
    factor = 0.5 * (3.0 * identity - growing)
    growing = jnp.dot(growing, factor, precision=lax.Precision.HIGHEST)
    inverse_part = factor
    for repeat in range(NS_ITERS - 1):
        factor = 0.5 * (3.0 * identity - jnp.dot(inverse_part, growing, precision=lax.Precision.HIGHEST))
        if repeat < NS_ITERS - 2:
            growing = jnp.dot(growing, factor, precision=lax.Precision.HIGHEST)
        inverse_part = jnp.dot(factor, inverse_part, precision=lax.Precision.HIGHEST)
    return inverse_part

def analyse(local_domain_grid_points, neighbours, tile_width):
    members = local_domain_grid_points.shape[0]
    ensemble_dispersion = jnp.transpose(neighbours[:, :members, :], (1, 0, 2)).reshape(members, -1)
    innovation = neighbours[:, members, :].astype(jnp.float32).reshape(-1)
    weighted = neighbours[:, members + 1, :].astype(jnp.float32)
    column = neighbours[:, members + 2, :].astype(jnp.float32)
    offsets = (jnp.arange(3, dtype=jnp.float32) - 1.0)[:, None] * tile_width
    distance = (column + offsets - 0.5 * (tile_width - 1)) / tile_width
    tapered = (weighted * jnp.exp(-0.5 * distance * distance)).reshape(-1)
    scaled_high, scaled_low = split_parts(ensemble_dispersion.astype(jnp.float32) * tapered[None, :])
    contract = (((1,), (1,)), ((), ()))
    gram = lax.dot_general(ensemble_dispersion, scaled_high, contract, preferred_element_type=jnp.float32)
    gram = gram + lax.dot_general(ensemble_dispersion, scaled_low, contract, preferred_element_type=jnp.float32)
    driver_high, driver_low = split_parts(tapered * innovation)
    forcing = jnp.dot(ensemble_dispersion, driver_high, preferred_element_type=jnp.float32)
    forcing = forcing + jnp.dot(ensemble_dispersion, driver_low, preferred_element_type=jnp.float32)
    identity = jnp.eye(members, dtype=jnp.float32)
    system = (members - 1.0) * identity + gram
    scaling = 0.5 * jnp.sqrt(jnp.sum(system * system))
    inverse_root = newton_schulz(system / scaling, identity) / jnp.sqrt(scaling)
    inner = jnp.dot(inverse_root, forcing, precision=lax.Precision.HIGHEST)
    average_weight_vector = jnp.dot(inverse_root, inner, precision=lax.Precision.HIGHEST)
    transform = (jnp.sqrt(members - 1.0) * inverse_root + average_weight_vector[:, None]).astype(jnp.bfloat16)
    as_float = local_domain_grid_points.astype(jnp.float32)
    state_mean = lax.optimization_barrier(jnp.mean(as_float, axis=0))
    deviation = (as_float - state_mean[None, :]).astype(jnp.bfloat16)
    updated = lax.dot_general(transform, deviation, (((0,), (0,)), ((), ())), preferred_element_type=jnp.float32)
    return (updated + state_mean[None, :]).astype(jnp.bfloat16)

def reference(ensemble, sweep_cfl_ratios, obs_cell, measurements_per_block, obs_value, obs_weight):
    member_grids = ensemble.astype(jnp.float32)
    for repeat in range(2):
        member_grids = advance(member_grids, sweep_cfl_ratios)
    background = member_grids.astype(jnp.bfloat16)
    band_rows = NY // N_MEM
    patch_total = N_MEM * N_TILE
    cell_table = obs_cell.reshape(N_MEM, N_TILE, OBS)
    value_table = obs_value.reshape(N_MEM, N_TILE, OBS)
    weight_table = obs_weight.reshape(N_MEM, N_TILE, OBS)

    def extract(index):
        band_position = index // N_TILE
        tile_index = index % N_TILE
        starts = (jnp.int32(0), (band_position * band_rows).astype(jnp.int32), (tile_index * BX).astype(jnp.int32))
        piece = lax.dynamic_slice(background, starts, (K, band_rows, BX))
        return piece.reshape(K, band_rows * BX)

    def block_of(index):
        band_position = index // N_TILE
        tile_index = index % N_TILE
        return observe(extract(index), cell_table[band_position, tile_index], measurements_per_block[band_position, tile_index], value_table[band_position, tile_index], weight_table[band_position, tile_index], BX)
    indices = jnp.arange(patch_total, dtype=jnp.int32)
    blocks = lax.map(block_of, indices).reshape(N_MEM, N_TILE, K + 3, OBS)

    def analyse_at(index):
        band_position = index // N_TILE
        tile_index = index % N_TILE
        lower = blocks[band_position, (tile_index + N_TILE - 1) % N_TILE]
        upper = blocks[band_position, (tile_index + 1) % N_TILE]
        neighbours = jnp.stack([lower, blocks[band_position, tile_index], upper])
        return analyse(extract(index), neighbours, BX)
    analysed = lax.map(analyse_at, indices)
    analysed = analysed.reshape(N_MEM, N_TILE, K, band_rows, BX).transpose(2, 0, 3, 1, 4).reshape(K, NY, NX)
    member_grids = advance(analysed.astype(jnp.float32), sweep_cfl_ratios)
    return member_grids.astype(jnp.bfloat16)
```

```python
import functools
import math

import jax
import jax.numpy as jnp
from jax import lax
from jax.experimental import pallas as pl
from jax.experimental.pallas import tpu as pltpu
from jax.sharding import PartitionSpec as P

MESH = pl.DeviceIdType.MESH
PAD = 8
F32, BF16 = jnp.float32, jnp.bfloat16


def minmod(ahead, behind):
    smaller = jnp.where(jnp.abs(ahead) < jnp.abs(behind), ahead, behind)
    return jnp.where(ahead * behind > 0.0, smaller, 0.0)


def flux_of(number, ahead, middle, behind):
    slope = minmod(ahead - middle, middle - behind)
    return number * (middle + (0.5 * (1.0 - number)) * slope)


def advance(field, flux, swept, cfl, store):
    rows, width = swept.shape[0], swept.shape[1]
    for j in range(rows):
        middle = field[j, PAD : PAD + width]
        values = flux_of(
            cfl[0, j],
            field[j, PAD + 1 : PAD + 1 + width],
            middle,
            field[j, PAD - 1 : PAD - 1 + width],
        )
        flux[j, PAD : PAD + width] = values
        swept[j] = middle - (values - flux[j, PAD - 1 : PAD - 1 + width])

    def across(j):
        return flux_of(cfl[1, j], swept[(j + 1) % rows], swept[j], swept[(j - 1) % rows])

    before = across(rows - 1)
    for j in range(rows):
        values = across(j)
        store(j, swept[j] - (values - before))
        before = values


def split(values):
    high = values.astype(BF16)
    return high, (values - high.astype(F32)).astype(BF16)


def dot(left, right, contract=((1,), (0,))):
    return lax.dot_general(left, right, (contract, ((), ())), preferred_element_type=F32)


def picker_of(cells, cell_row):
    places = lax.broadcasted_iota(jnp.int32, (cells, cell_row.shape[1]), 0).astype(F32)
    return jnp.where(places == cell_row, 1.0, 0.0).astype(BF16)


def lane_sum(values):
    return jnp.sum(values, axis=1, keepdims=True)


def block_terms(sampled, meta, offset, tile_width):
    members = sampled.shape[1]
    columns = jnp.transpose(meta)
    weighted, value, column = columns[:, 1:2], columns[:, 2:3], columns[:, 3:4]
    distance = (column + offset * tile_width - 0.5 * (tile_width - 1)) / tile_width
    taper = weighted * jnp.exp(-0.5 * distance * distance)
    mean = lane_sum(sampled) * (1.0 / members)
    spread = (sampled - mean).astype(BF16)
    innovation = (value - mean).astype(BF16).astype(F32)
    as_float = spread.astype(F32)
    forcing = jnp.sum(as_float * (taper * innovation), axis=0, keepdims=True)
    high, low = split(as_float * taper)
    flipped = jnp.transpose(spread)
    gram = dot(jnp.concatenate([flipped, flipped], 1), jnp.concatenate([high, low], 0))
    return gram, forcing


def transform_rows(gram, forcing):
    members = gram.shape[0]
    across = lax.broadcasted_iota(jnp.int32, (members, members), 1)
    on_diagonal = lax.broadcasted_iota(jnp.int32, (members, members), 0) == across
    system = gram + jnp.where(on_diagonal, members - 1.0, 0.0)
    total = jnp.sum(lane_sum(system * system), axis=0, keepdims=True)
    scaling = 0.5 * jnp.sqrt(total)
    a = (members - 1.0) / scaling
    x = gram * (1.0 / scaling)
    factor = (1.0 / 16.0) / jnp.sqrt(scaling)
    c0 = (36.0 + a * (-39.0 + a * (27.0 + a * (-9.0 + a)))) * factor
    c1 = (-39.0 + a * (54.0 + a * (-27.0 + 4.0 * a))) * factor
    c2 = (27.0 + a * (-27.0 + 6.0 * a)) * factor
    c3 = (-9.0 + 4.0 * a) * factor
    rounded = x.astype(BF16)
    second = dot(rounded, rounded)
    higher = dot(second.astype(BF16), (c3 * x + factor * second).astype(BF16))
    root = c1 * x + c2 * second + higher + jnp.where(on_diagonal, c0, 0.0)
    inner = lane_sum(root * forcing)
    weights = jnp.sum(root * inner, axis=0, keepdims=True)
    return (math.sqrt(members - 1.0) * root + weights).astype(BF16)


def kernel(
    nm, nt,
    ens_hbm, cfl_hbm, cell_hbm, count_hbm, value_hbm, weight_hbm, out,
    ens, cfl, cell, count, value, weight, stage,
    field, flux, swept, edge, halo, meta, bg, meta_mem, meta_tile, patch, smp_out, smp_in,
    ana, ana_edge, fin, fin_halo, local_sem, send_sem, recv_sem,
):
    mine, rows, width = ens.shape
    band = rows // nm
    cells = band * width
    m, t = lax.axis_index("mem"), lax.axis_index("tile")
    right, left = lax.rem(t + 1, nt), lax.rem(t + nt - 1, nt)
    up = [lax.rem(m + k, nm) for k in range(nm)]
    down = [lax.rem(m + nm - k, nm) for k in range(nm)]

    barrier = pltpu.get_barrier_semaphore()
    others = [(up[k], t) for k in range(1, nm)] + [(m, right), (m, left)]
    for other in others:
        pl.semaphore_signal(barrier, inc=1, device_id=other, device_id_type=MESH)
    loads = [
        pltpu.make_async_copy(src, dst, local_sem.at[n])
        for n, (src, dst) in enumerate(
            [
                (ens_hbm, ens), (cfl_hbm, cfl), (cell_hbm, cell),
                (count_hbm, count), (value_hbm, value), (weight_hbm, weight),
            ]
        )
    ]
    for load in loads:
        load.start()

    used = [0]

    def send(src, dst, device):
        n = used[0]
        used[0] += 1
        copy = pltpu.make_async_remote_copy(
            src_ref=src, dst_ref=dst, send_sem=send_sem.at[n], recv_sem=recv_sem.at[n],
            device_id=device, device_id_type=MESH,
        )
        copy.start()
        return copy

    start = 2 * PAD
    end = start + width
    for load in loads:
        load.wait()
    cells_row = cell[...].astype(F32)
    live = lax.broadcasted_iota(jnp.int32, cells_row.shape, 1) < count[0, 0]
    meta[0:1] = cells_row
    meta[1:2] = jnp.where(live, weight[...], 0.0).astype(BF16).astype(F32)
    meta[2:3] = value[...]
    meta[3:4] = cells_row - width * jnp.floor(cells_row * (1.0 / width))
    meta[4:8] = jnp.zeros((4, cells_row.shape[1]), F32)
    stage[...] = ens[...].astype(F32)
    for i in range(rows // 2):
        pair = [jnp.transpose(stage[:, 2 * i + n, :]) for n in range(2)]
        for n in range(2):
            field[2 * i + n, start:end] = pair[n]
        edge[0, i] = jnp.concatenate([p[width - PAD :] for p in pair], 0).astype(BF16)
        edge[1, i] = jnp.concatenate([p[:PAD] for p in pair], 0).astype(BF16)
    pl.semaphore_wait(barrier, len(others))

    halo_copies = [send(edge.at[0], halo.at[0], (m, right)), send(edge.at[1], halo.at[1], (m, left))]
    meta_copies = [send(meta, meta_mem.at[k], (up[k], t)) for k in range(1, nm)]
    tile_copies = [
        send(meta, meta_tile.at[0], (m, right)),
        send(meta, meta_tile.at[1], (m, left)),
    ]
    for copy in halo_copies:
        copy.wait()
    for i in range(rows // 2):
        for side, place in ((0, PAD), (1, end)):
            both = halo[side, i].astype(F32)
            field[2 * i, place : place + PAD] = both[:PAD]
            field[2 * i + 1, place : place + PAD] = both[PAD:]

    def keep(j, values):
        field[j, PAD : PAD + values.shape[0]] = values

    def keep_background(j, values):
        bg[j // band, j % band] = values[PAD : PAD + width].astype(BF16)

    advance(field, flux, swept, cfl, keep)
    advance(field, flux, swept, cfl, keep_background)

    for copy in meta_copies:
        copy.wait()
    smp_copies, patch_copies = [], []
    for k in [*range(1, nm), 0]:
        source = meta if k == 0 else meta_mem.at[nm - k]
        picker = picker_of(cells, source[0:1])
        band_cells = bg[up[k]].reshape(cells, mine)
        smp_out[k] = dot(picker, band_cells, ((0,), (0,))).astype(BF16)
        smp_copies.append(
            (
                send(smp_out.at[k], smp_in.at[0, k], (up[k], right)),
                send(smp_out.at[k], smp_in.at[1, k], (up[k], left)),
            )
        )
        if k:
            patch_copies.append(send(bg.at[up[k]], patch.at[k], (up[k], t)))
    for copy in patch_copies:
        copy.wait()
    pieces = [bg[m].reshape(cells, mine)]
    pieces += [patch[k].reshape(cells, mine) for k in range(1, nm)]
    whole = jnp.concatenate(pieces, 1)
    own = dot(picker_of(cells, meta[0:1]), whole, ((0,), (0,)))
    as_float = whole.astype(F32)
    state_mean = lane_sum(as_float) * (1.0 / as_float.shape[1])
    deviation = (as_float - state_mean).astype(BF16)
    gram, forcing = block_terms(own, meta[...], 0.0, width)
    for side in range(2):
        tile_copies[side].wait()
        for pair in smp_copies:
            pair[side].wait()
        sampled = jnp.concatenate([smp_in[side, k] for k in range(nm)], 1).astype(F32)
        more, force = block_terms(sampled, meta_tile[side], 2.0 * side - 1.0, width)
        gram, forcing = gram + more, forcing + force
    transform = transform_rows(gram, forcing)
    updated = dot(deviation, transform, ((1,), (1,))) + state_mean
    last = []
    for k in range(nm):
        piece = updated[:, k * mine : (k + 1) * mine]
        for side, place in ((0, width - PAD), (1, 0)):
            ana_edge[side, k] = jnp.concatenate(
                [piece[r * width + place : r * width + place + PAD] for r in range(band)], 0
            ).astype(BF16)
            last.append(
                send(
                    ana_edge.at[side, k], fin_halo.at[side, m],
                    (down[k], left if side else right),
                )
            )
        ana[k] = piece.astype(BF16).reshape(band, width, mine)
        if k:
            last.append(send(ana.at[k], fin.at[m], (down[k], t)))
    fin[m] = ana[0]
    for copy in last:
        copy.wait()
    for j in range(rows):
        b, r = j // band, j % band
        field[j, start:end] = fin[b, r].astype(F32)
        rim = slice(r * PAD, (r + 1) * PAD)
        field[j, PAD:start] = fin_halo[0, b].astype(F32)[rim]
        field[j, end : end + PAD] = fin_halo[1, b].astype(F32)[rim]

    def keep_forecast(j, values):
        out[j] = values[PAD : PAD + width].astype(BF16)

    advance(field, flux, swept, cfl, keep_forecast)


def on_device(nm, nt, ensemble, *others):
    mine, rows, width = ensemble.shape
    band, slots = rows // nm, others[1].shape[1]
    copies = 2 + (nm - 1) + 2 + (nm - 1) + 2 * nm + (nm - 1) + 2 * nm
    one_row = pltpu.VMEM((1, slots), F32)
    forecast = pl.pallas_call(
        functools.partial(kernel, nm, nt),
        out_shape=jax.ShapeDtypeStruct((rows, width, mine), BF16),
        in_specs=[pl.BlockSpec(memory_space=pl.ANY)] * 6,
        out_specs=pl.BlockSpec(memory_space=pltpu.VMEM),
        scratch_shapes=[
            pltpu.VMEM(ensemble.shape, BF16),
            pltpu.SMEM(others[0].shape, F32),
            pltpu.VMEM((1, slots), jnp.int32),
            pltpu.SMEM((1, 1), jnp.int32),
            one_row,
            one_row,
            pltpu.VMEM(ensemble.shape, F32),
            pltpu.VMEM((rows, width + 4 * PAD, mine), F32),
            pltpu.VMEM((rows, width + 4 * PAD, mine), F32),
            pltpu.VMEM((rows, width + 2 * PAD, mine), F32),
            pltpu.VMEM((2, rows // 2, 2 * PAD, mine), BF16),
            pltpu.VMEM((2, rows // 2, 2 * PAD, mine), BF16),
            pltpu.VMEM((8, slots), F32),
            pltpu.VMEM((nm, band, width, mine), BF16),
            pltpu.VMEM((nm, 8, slots), F32),
            pltpu.VMEM((2, 8, slots), F32),
            pltpu.VMEM((nm, band, width, mine), BF16),
            pltpu.VMEM((nm, slots, mine), BF16),
            pltpu.VMEM((2, nm, slots, mine), BF16),
            pltpu.VMEM((nm, band, width, mine), BF16),
            pltpu.VMEM((2, nm, band * PAD, mine), BF16),
            pltpu.VMEM((nm, band, width, mine), BF16),
            pltpu.VMEM((2, nm, band * PAD, mine), BF16),
            pltpu.SemaphoreType.DMA((6,)),
            pltpu.SemaphoreType.DMA((copies,)),
            pltpu.SemaphoreType.DMA((copies,)),
        ],
        compiler_params=pltpu.CompilerParams(
            collective_id=0, has_side_effects=True, vmem_limit_bytes=60 * 1024 * 1024
        ),
    )(ensemble, *others)
    return jnp.transpose(forecast, (2, 0, 1))


def solution(mesh):
    in_specs = (
        P("mem", None, "tile"),
        P(),
        P("mem", "tile"),
        P("mem", "tile"),
        P("mem", "tile"),
        P("mem", "tile"),
    )
    out_specs = P("mem", None, "tile")
    body = functools.partial(on_device, mesh.shape["mem"], mesh.shape["tile"])
    return jax.shard_map(
        body, mesh=mesh, in_specs=in_specs, out_specs=out_specs, check_vma=False
    )
```

```python
import functools
import math

import jax
import jax.numpy as jnp
from jax import lax
from jax.experimental import pallas as pl
from jax.experimental.pallas import tpu as pltpu
from jax.sharding import PartitionSpec as P

MESH = pl.DeviceIdType.MESH
PAD = 8
F32, BF16 = jnp.float32, jnp.bfloat16


def minmod(ahead, behind):
    smaller = jnp.where(jnp.abs(ahead) < jnp.abs(behind), ahead, behind)
    return jnp.where(ahead * behind > 0.0, smaller, 0.0)


def flux_of(number, ahead, middle, behind):
    slope = minmod(ahead - middle, middle - behind)
    return number * (middle + (0.5 * (1.0 - number)) * slope)


def advance(field, flux, swept, cfl, store):
    rows, width = swept.shape[0], swept.shape[1]
    for j in range(rows):
        middle = field[j, PAD : PAD + width]
        values = flux_of(
            cfl[0, j],
            field[j, PAD + 1 : PAD + 1 + width],
            middle,
            field[j, PAD - 1 : PAD - 1 + width],
        )
        flux[j, PAD : PAD + width] = values
        swept[j] = middle - (values - flux[j, PAD - 1 : PAD - 1 + width])

    def across(j):
        return flux_of(cfl[1, j], swept[(j + 1) % rows], swept[j], swept[(j - 1) % rows])

    before = across(rows - 1)
    for j in range(rows):
        values = across(j)
        store(j, swept[j] - (values - before))
        before = values


def split(values):
    high = values.astype(BF16)
    return high, (values - high.astype(F32)).astype(BF16)


def dot(left, right, contract=((1,), (0,))):
    return lax.dot_general(left, right, (contract, ((), ())), preferred_element_type=F32)


def picker_of(cells, cell_row):
    places = lax.broadcasted_iota(jnp.int32, (cells, cell_row.shape[1]), 0).astype(F32)
    return jnp.where(places == cell_row, 1.0, 0.0).astype(BF16)


def lane_sum(values):
    return jnp.sum(values, axis=1, keepdims=True)


def block_terms(sampled, meta, offset, tile_width):
    members = sampled.shape[1]
    columns = jnp.transpose(meta)
    weighted, value, column = columns[:, 1:2], columns[:, 2:3], columns[:, 3:4]
    distance = (column + offset * tile_width - 0.5 * (tile_width - 1)) / tile_width
    taper = weighted * jnp.exp(-0.5 * distance * distance)
    mean = lane_sum(sampled) * (1.0 / members)
    spread = (sampled - mean).astype(BF16)
    innovation = (value - mean).astype(BF16).astype(F32)
    as_float = spread.astype(F32)
    forcing = jnp.sum(as_float * (taper * innovation), axis=0, keepdims=True)
    high, low = split(as_float * taper)
    flipped = jnp.transpose(spread)
    gram = dot(jnp.concatenate([flipped, flipped], 1), jnp.concatenate([high, low], 0))
    return gram, forcing


def transform_rows(gram, forcing):
    members = gram.shape[0]
    across = lax.broadcasted_iota(jnp.int32, (members, members), 1)
    on_diagonal = lax.broadcasted_iota(jnp.int32, (members, members), 0) == across
    system = gram + jnp.where(on_diagonal, members - 1.0, 0.0)
    total = jnp.sum(lane_sum(system * system), axis=0, keepdims=True)
    scaling = 0.5 * jnp.sqrt(total)
    a = (members - 1.0) / scaling
    x = gram * (1.0 / scaling)
    factor = (1.0 / 16.0) / jnp.sqrt(scaling)
    c0 = (36.0 + a * (-39.0 + a * (27.0 + a * (-9.0 + a)))) * factor
    c1 = (-39.0 + a * (54.0 + a * (-27.0 + 4.0 * a))) * factor
    c2 = (27.0 + a * (-27.0 + 6.0 * a)) * factor
    c3 = (-9.0 + 4.0 * a) * factor
    rounded = x.astype(BF16)
    second = dot(rounded, rounded)
    higher = dot(second.astype(BF16), (c3 * x + factor * second).astype(BF16))
    root = c1 * x + c2 * second + higher + jnp.where(on_diagonal, c0, 0.0)
    inner = lane_sum(root * forcing)
    weights = jnp.sum(root * inner, axis=0, keepdims=True)
    return (math.sqrt(members - 1.0) * root + weights).astype(BF16)


def kernel(
    nm, nt,
    ens_hbm, cfl_hbm, cell_hbm, count_hbm, value_hbm, weight_hbm, out,
    ens, cfl, cell, count, value, weight, stage,
    field, flux, swept, inner, rim, rim_flux, rim_swept, edge, halo, meta, bg, meta_mem, meta_tile, patch, smp_out, smp_in,
    ana, ana_edge, fin, fin_halo, local_sem, send_sem, recv_sem,
):
    mine, rows, width = ens.shape
    band = rows // nm
    cells = band * width
    m, t = lax.axis_index("mem"), lax.axis_index("tile")
    right, left = lax.rem(t + 1, nt), lax.rem(t + nt - 1, nt)
    up = [lax.rem(m + k, nm) for k in range(nm)]
    down = [lax.rem(m + nm - k, nm) for k in range(nm)]

    barrier = pltpu.get_barrier_semaphore()
    others = [(up[k], t) for k in range(1, nm)] + [(m, right), (m, left)]
    for other in others:
        pl.semaphore_signal(barrier, inc=1, device_id=other, device_id_type=MESH)
    loads = [
        pltpu.make_async_copy(src, dst, local_sem.at[n])
        for n, (src, dst) in enumerate(
            [
                (ens_hbm, ens), (cfl_hbm, cfl), (cell_hbm, cell),
                (count_hbm, count), (value_hbm, value), (weight_hbm, weight),
            ]
        )
    ]
    for load in loads:
        load.start()

    used = [0]

    def send(src, dst, device):
        n = used[0]
        used[0] += 1
        copy = pltpu.make_async_remote_copy(
            src_ref=src, dst_ref=dst, send_sem=send_sem.at[n], recv_sem=recv_sem.at[n],
            device_id=device, device_id_type=MESH,
        )
        copy.start()
        return copy

    start = 2 * PAD
    end = start + width
    for load in loads:
        load.wait()
    cells_row = cell[...].astype(F32)
    live = lax.broadcasted_iota(jnp.int32, cells_row.shape, 1) < count[0, 0]
    meta[0:1] = cells_row
    meta[1:2] = jnp.where(live, weight[...], 0.0).astype(BF16).astype(F32)
    meta[2:3] = value[...]
    meta[3:4] = cells_row - width * jnp.floor(cells_row * (1.0 / width))
    meta[4:8] = jnp.zeros((4, cells_row.shape[1]), F32)
    stage[...] = ens[...].astype(F32)
    for i in range(rows // 2):
        pair = [jnp.transpose(stage[:, 2 * i + n, :]) for n in range(2)]
        for n in range(2):
            field[2 * i + n, start:end] = pair[n]
            rim[2 * i + n, start : start + 2 * PAD] = pair[n][: 2 * PAD]
            rim[2 * i + n, start + 2 * PAD : start + 4 * PAD] = pair[n][width - 2 * PAD :]
        edge[0, i] = jnp.concatenate([p[width - PAD :] for p in pair], 0).astype(BF16)
        edge[1, i] = jnp.concatenate([p[:PAD] for p in pair], 0).astype(BF16)
    pl.semaphore_wait(barrier, len(others))

    halo_copies = [send(edge.at[0], halo.at[0], (m, right)), send(edge.at[1], halo.at[1], (m, left))]
    meta_copies = [send(meta, meta_mem.at[k], (up[k], t)) for k in range(1, nm)]
    tile_copies = [
        send(meta, meta_tile.at[0], (m, right)),
        send(meta, meta_tile.at[1], (m, left)),
    ]

    def keep(ref):
        def store(j, values):
            ref[j, PAD : PAD + values.shape[0]] = values

        return store

    def keep_inner(j, values):
        inner[j] = values[PAD : PAD + width]

    def keep_background(j, values):
        bg[j // band, j % band] = jnp.concatenate(
            [values[PAD : 2 * PAD], inner[j, PAD : width - PAD], values[4 * PAD : 5 * PAD]], 0
        ).astype(BF16)

    advance(field, flux, swept, cfl, keep(field))
    advance(field, flux, swept, cfl, keep_inner)
    for copy in halo_copies:
        copy.wait()
    for i in range(rows // 2):
        for side, place in ((0, PAD), (1, start + 4 * PAD)):
            both = halo[side, i].astype(F32)
            rim[2 * i, place : place + PAD] = both[:PAD]
            rim[2 * i + 1, place : place + PAD] = both[PAD:]
    advance(rim, rim_flux, rim_swept, cfl, keep(rim))
    advance(rim, rim_flux, rim_swept, cfl, keep_background)

    for copy in meta_copies:
        copy.wait()
    smp_copies, patch_copies = [], []
    for k in [*range(1, nm), 0]:
        source = meta if k == 0 else meta_mem.at[nm - k]
        picker = picker_of(cells, source[0:1])
        band_cells = bg[up[k]].reshape(cells, mine)
        smp_out[k] = dot(picker, band_cells, ((0,), (0,))).astype(BF16)
        smp_copies.append(
            (
                send(smp_out.at[k], smp_in.at[0, k], (up[k], right)),
                send(smp_out.at[k], smp_in.at[1, k], (up[k], left)),
            )
        )
        if k:
            patch_copies.append(send(bg.at[up[k]], patch.at[k], (up[k], t)))
    for copy in patch_copies:
        copy.wait()
    pieces = [bg[m].reshape(cells, mine)]
    pieces += [patch[k].reshape(cells, mine) for k in range(1, nm)]
    whole = jnp.concatenate(pieces, 1)
    own = dot(picker_of(cells, meta[0:1]), whole, ((0,), (0,)))
    as_float = whole.astype(F32)
    state_mean = lane_sum(as_float) * (1.0 / as_float.shape[1])
    deviation = (as_float - state_mean).astype(BF16)
    gram, forcing = block_terms(own, meta[...], 0.0, width)
    for side in range(2):
        tile_copies[side].wait()
        for pair in smp_copies:
            pair[side].wait()
        sampled = jnp.concatenate([smp_in[side, k] for k in range(nm)], 1).astype(F32)
        more, force = block_terms(sampled, meta_tile[side], 2.0 * side - 1.0, width)
        gram, forcing = gram + more, forcing + force
    transform = transform_rows(gram, forcing)
    updated = dot(deviation, transform, ((1,), (1,))) + state_mean
    last = []
    for k in range(nm):
        piece = updated[:, k * mine : (k + 1) * mine]
        for side, place in ((0, width - PAD), (1, 0)):
            ana_edge[side, k] = jnp.concatenate(
                [piece[r * width + place : r * width + place + PAD] for r in range(band)], 0
            ).astype(BF16)
            last.append(
                send(
                    ana_edge.at[side, k], fin_halo.at[side, m],
                    (down[k], left if side else right),
                )
            )
        ana[k] = piece.astype(BF16).reshape(band, width, mine)
        if k:
            last.append(send(ana.at[k], fin.at[m], (down[k], t)))
    fin[m] = ana[0]
    for copy in last:
        copy.wait()
    for j in range(rows):
        b, r = j // band, j % band
        field[j, start:end] = fin[b, r].astype(F32)
        rim = slice(r * PAD, (r + 1) * PAD)
        field[j, PAD:start] = fin_halo[0, b].astype(F32)[rim]
        field[j, end : end + PAD] = fin_halo[1, b].astype(F32)[rim]

    def keep_forecast(j, values):
        stage[:, j, :] = jnp.transpose(values[PAD : PAD + width])

    advance(field, flux, swept, cfl, keep_forecast)
    out[...] = stage[...].astype(BF16)


def on_device(nm, nt, ensemble, *others):
    mine, rows, width = ensemble.shape
    band, slots = rows // nm, others[1].shape[1]
    copies = 2 + (nm - 1) + 2 + (nm - 1) + 2 * nm + (nm - 1) + 2 * nm
    one_row = pltpu.VMEM((1, slots), F32)
    return pl.pallas_call(
        functools.partial(kernel, nm, nt),
        out_shape=jax.ShapeDtypeStruct(ensemble.shape, BF16),
        in_specs=[pl.BlockSpec(memory_space=pl.ANY)] * 6,
        out_specs=pl.BlockSpec(memory_space=pltpu.VMEM),
        scratch_shapes=[
            pltpu.VMEM(ensemble.shape, BF16),
            pltpu.SMEM(others[0].shape, F32),
            pltpu.VMEM((1, slots), jnp.int32),
            pltpu.SMEM((1, 1), jnp.int32),
            one_row,
            one_row,
            pltpu.VMEM(ensemble.shape, F32),
            pltpu.VMEM((rows, width + 4 * PAD, mine), F32),
            pltpu.VMEM((rows, width + 4 * PAD, mine), F32),
            pltpu.VMEM((rows, width + 2 * PAD, mine), F32),
            pltpu.VMEM((rows, width, mine), F32),
            pltpu.VMEM((rows, 8 * PAD, mine), F32),
            pltpu.VMEM((rows, 8 * PAD, mine), F32),
            pltpu.VMEM((rows, 6 * PAD, mine), F32),
            pltpu.VMEM((2, rows // 2, 2 * PAD, mine), BF16),
            pltpu.VMEM((2, rows // 2, 2 * PAD, mine), BF16),
            pltpu.VMEM((8, slots), F32),
            pltpu.VMEM((nm, band, width, mine), BF16),
            pltpu.VMEM((nm, 8, slots), F32),
            pltpu.VMEM((2, 8, slots), F32),
            pltpu.VMEM((nm, band, width, mine), BF16),
            pltpu.VMEM((nm, slots, mine), BF16),
            pltpu.VMEM((2, nm, slots, mine), BF16),
            pltpu.VMEM((nm, band, width, mine), BF16),
            pltpu.VMEM((2, nm, band * PAD, mine), BF16),
            pltpu.VMEM((nm, band, width, mine), BF16),
            pltpu.VMEM((2, nm, band * PAD, mine), BF16),
            pltpu.SemaphoreType.DMA((6,)),
            pltpu.SemaphoreType.DMA((copies,)),
            pltpu.SemaphoreType.DMA((copies,)),
        ],
        compiler_params=pltpu.CompilerParams(
            collective_id=0, has_side_effects=True, vmem_limit_bytes=60 * 1024 * 1024
        ),
    )(ensemble, *others)


def solution(mesh):
    in_specs = (
        P("mem", None, "tile"),
        P(),
        P("mem", "tile"),
        P("mem", "tile"),
        P("mem", "tile"),
        P("mem", "tile"),
    )
    out_specs = P("mem", None, "tile")
    body = functools.partial(on_device, mesh.shape["mem"], mesh.shape["tile"])
    return jax.shard_map(
        body, mesh=mesh, in_specs=in_specs, out_specs=out_specs, check_vma=False
    )
```
